512 devices in a mesh: group: 16 (over z), sub: 32 (over x, y, core).
Axes of the slice: x: 4, y: 4, z: 16, core: 2. Of those that a mesh axis runs over, the one named last changes fastest.
Arguments:
- couplings: float32 [512, 6, 384, 384], P(('group', 'sub')), may hold values from -0.3125 to 0.3125
- mode_rows: float32 [786432, 128], P(('group', 'sub')), may hold values from -1.5 to 1.5
- coarse_basis: float32 [65536, 256], P(('group', 'sub')), may hold values from -0.09375 to 0.09375
- stiffness: float32 [512, 1536], P(('group', 'sub')), may hold values from 0.005 to 0.05
- own_face: int32 [512, 6], P(('group', 'sub')), may hold values from 0 to 3, as said below
- neighbour_face: int32 [512, 6], P(('group', 'sub')), may hold values from 0 to 3, as said below
- present: int32 [512, 6], P(('group', 'sub')), may hold values from 0 to 1, as said below
Outputs:
- coarse_blocks: float32 [512, 7, 128, 128], P(('group', 'sub'))
- coarse_group: float32 [16, 3, 256, 256], P('group', None, 'sub')
The draws below stay inside these ranges and needn't reach their ends.
Inputs may be any that keep to these rules, and one draw needn't show every extreme that they name: `own_face`: face block index of the subdomain's own unknowns toward each direction. Wherever present is 1, neighbour_face[d, k] equals own_face of the neighbour n(d, k) at the opposite direction (0 and 1, 2 and 3, 4 and 5 are opposite). `present`: 0 wherever the neighbour lies outside the group's plane of 4 columns and 8 rows or outside the groups, and on broken couplings; a coupling is intact on both sides or on neither.
All inputs are finite; a program needn't handle non-finite values.
Results may differ from the reference program's by a relative error of at most 0.0003.
Values sent between devices are 32-bit elements; how exact they have to be, the bound alone decides.
No kernel may reach another device: no remote copies, remote signals or barrier semaphores. Data moves between devices by JAX's collectives and lax.ppermute only.
A program may use at most 64 MiB of HBM per device.

```python
import math
import jax
import jax.numpy as jnp
from jax import lax

BLOCK = 384
FACES = 4
UNKNOWNS = 1536
MODES = 128
MODES2 = 256
DIRS = 6
SUB_ROW = 4
SUBS = 32
GROUPS = 16
SUBDOMAINS = 512


def layout(key):
    index = jnp.arange(SUBDOMAINS, dtype=jnp.int32)
    group_of = index // SUBS
    within = index % SUBS
    row_of = within // SUB_ROW
    column = within % SUB_ROW
    faces = jax.random.randint(jax.random.fold_in(key, 11), (SUBDOMAINS, DIRS), 0, FACES, dtype=jnp.int32)
    intact = jax.random.randint(jax.random.fold_in(key, 12), (SUBDOMAINS, 3), 0, 4, dtype=jnp.int32) != 0
    upward = jnp.stack([column + 1 < SUB_ROW, row_of + 1 < SUBS // SUB_ROW, group_of + 1 < GROUPS], axis=1) & intact
    strides = jnp.array([1, SUB_ROW, SUBS], jnp.int32)
    below_index = jnp.clip(index[:, None] - strides[None, :], 0, SUBDOMAINS - 1)
    has_below = jnp.stack([column > 0, row_of > 0, group_of > 0], axis=1)
    downward = has_below & jnp.take_along_axis(upward, below_index, axis=0)
    present = jnp.stack([downward[:, 0], upward[:, 0], downward[:, 1], upward[:, 1], downward[:, 2], upward[:, 2]], axis=1).astype(jnp.int32)
    offsets = jnp.array([-1, 1, -SUB_ROW, SUB_ROW, -SUBS, SUBS], jnp.int32)
    neighbour = jnp.clip(index[:, None] + offsets[None, :], 0, SUBDOMAINS - 1)
    opposite = jnp.array([1, 0, 3, 2, 5, 4], jnp.int32)
    neighbour_faces = faces[neighbour, jnp.broadcast_to(opposite[None, :], (SUBDOMAINS, DIRS))]
    return (faces, neighbour_faces.astype(jnp.int32), present)


def draw_own_face(key, part):
    return layout(key)[0]


def draw_neighbour_face(key, part):
    return layout(key)[1]


def draw_present(key, part):
    return layout(key)[2]


def block_scale(key, extent, cuts, smallest, top_value):
    factor_of, own = 1.0, jax.random.fold_in(key, 6)
    for position, parts in cuts:
        heights = jnp.exp(jax.random.uniform(jax.random.fold_in(own, position), (parts,), jnp.float32, smallest / len(cuts), top_value / len(cuts)))
        factor_of = factor_of * jnp.repeat(heights, extent[position] // parts).reshape([-1 if axis == position else 1 for axis in range(len(extent))])
    return factor_of


def bell_draw(key, dims, scale, reach, split=(), held_as=jnp.bfloat16):
    values = scale * jax.random.normal(key, dims, jnp.float32)
    if split:
        values = values * block_scale(key, dims, split, -0.22, 0.18)
    return jnp.clip(values, -reach, reach).astype(held_as)


def setup_inputs(seed: int = 0) -> dict:
    arg_keys = jax.random.split(jax.random.key(seed), 8)
    return {
        "couplings": bell_draw(arg_keys[0], (SUBDOMAINS, DIRS, BLOCK, BLOCK), BLOCK ** -0.5, 0.3125, ((0, 512),), jnp.float32),
        "mode_rows": bell_draw(arg_keys[1], (SUBDOMAINS * UNKNOWNS, MODES), 0.25, 1.5, ((0, 512),), jnp.float32),
        "coarse_basis": bell_draw(arg_keys[2], (SUBDOMAINS * MODES, MODES2), (MODES * SUBS) ** -0.5, 0.09375, ((0, 512),), jnp.float32),
        "stiffness": jnp.clip(jnp.exp(math.log(0.05) - 2.3025851 * jax.random.uniform(arg_keys[3], (SUBDOMAINS, UNKNOWNS), jnp.float32) ** block_scale(arg_keys[3], (SUBDOMAINS, UNKNOWNS), ((0, 512),), -0.2, 0.2)), 0.005, 0.05),
        "own_face": draw_own_face(jax.random.fold_in(arg_keys[7], 71), 0),
        "neighbour_face": draw_neighbour_face(jax.random.fold_in(arg_keys[7], 71), 0),
        "present": draw_present(jax.random.fold_in(arg_keys[7], 71), 0),
    }


PRECISE = lax.Precision.HIGHEST


def matmul(left, right):
    return jnp.dot(left, right, precision=PRECISE, preferred_element_type=jnp.float32)


def transposed_product(left, right):
    return lax.dot_general(left, right, (((0,), (0,)), ((), ())), precision=PRECISE, preferred_element_type=jnp.float32)


def reference(couplings, mode_rows, coarse_basis, stiffness, own_face, neighbour_face, present):
    modes_all = mode_rows.reshape(SUBDOMAINS, UNKNOWNS, MODES)
    basis_all = coarse_basis.reshape(SUBDOMAINS, MODES, MODES2)
    offsets = jnp.array([-1, 1, -SUB_ROW, SUB_ROW, -SUBS, SUBS], jnp.int32)

    def per_subdomain(subdomain):
        own_modes = modes_all[subdomain]
        own_basis = basis_all[subdomain]
        block_list = []
        projected = []
        for direction in range(DIRS):
            neighbour = jnp.clip(subdomain + offsets[direction], 0, SUBDOMAINS - 1).astype(jnp.int32)
            own_part = lax.dynamic_slice_in_dim(own_modes, (own_face[subdomain, direction] * BLOCK).astype(jnp.int32), BLOCK, 0)
            far_part = lax.dynamic_slice_in_dim(modes_all[neighbour], (neighbour_face[subdomain, direction] * BLOCK).astype(jnp.int32), BLOCK, 0)
            weight = present[subdomain, direction].astype(jnp.float32)
            product = matmul(couplings[subdomain, direction], own_part)
            coarse_block = transposed_product(product, far_part) * weight
            block_list.append(coarse_block)
            projected.append(matmul(transposed_product(own_basis, coarse_block), basis_all[neighbour]))
        self_block = transposed_product(own_modes * stiffness[subdomain][:, None], own_modes)
        block_list.append(self_block)
        within = matmul(transposed_product(own_basis, self_block), own_basis)
        within = within + projected[0] + projected[1] + projected[2] + projected[3]
        return jnp.stack(block_list), jnp.stack([projected[4], within, projected[5]])

    blocks_out, terms_out = lax.map(per_subdomain, jnp.arange(SUBDOMAINS, dtype=jnp.int32))
    coarse_group = terms_out.reshape(GROUPS, SUBS, 3, MODES2, MODES2).sum(axis=1)
    return blocks_out, coarse_group
```

```python
import jax
import jax.numpy as jnp
from jax import lax
from jax.experimental import pallas as pl
from jax.experimental.pallas import tpu as pltpu
from jax.sharding import PartitionSpec as P

DIRS = 6
SUB_ROW = 4
SUBS = 32
GROUPS = 16
BLOCK = 384
MODES = 128
MODES2 = 256
PACKED = BLOCK + MODES2

EXCHANGES = (("row", 0), ("row", 1), ("group", 0), ("group", 1), ("column", 1), ("column", 0))


F32 = jnp.float32
BF16 = jnp.bfloat16
SMEM = pl.BlockSpec(memory_space=pltpu.SMEM)
VMEM = pl.BlockSpec(memory_space=pltpu.VMEM)


def swap_pairs(extent, stride, odd):
    pairs = []
    for low in range(odd, extent - 1, 2):
        pairs += [(low, low + 1), (low + 1, low)]
    return pairs


def exchange(packed, kind, odd):
    if kind == "group":
        return lax.ppermute(packed, "group", swap_pairs(GROUPS, 1, odd))
    pairs = []
    if kind == "row":
        for one, two in swap_pairs(SUBS // SUB_ROW, 1, odd):
            pairs += [(one * SUB_ROW + c, two * SUB_ROW + c) for c in range(SUB_ROW)]
    else:
        for one, two in swap_pairs(SUB_ROW, 1, odd):
            pairs += [(r * SUB_ROW + one, r * SUB_ROW + two) for r in range(SUBS // SUB_ROW)]
    return lax.ppermute(packed, "sub", pairs)


def slot_directions():
    sub, group = lax.axis_index("sub"), lax.axis_index("group")
    place = {
        "column": (lax.rem(sub, SUB_ROW), 0),
        "row": (lax.div(sub, SUB_ROW), 2),
        "group": (group, 4),
    }
    found = []
    for kind, odd in EXCHANGES:
        position, base = place[kind]
        found.append(base + 1 - lax.rem(position + odd, 2))
    return found


def split(x):
    high = x.astype(BF16)
    return high, (x - high.astype(F32)).astype(BF16)


def dot(a, b):
    return jnp.dot(a, b, preferred_element_type=F32)


def dot_wide(a, b):
    (a_high, a_low), (b_high, b_low) = a, b
    return dot(a_high, b_high) + (dot(a_high, b_low) + dot(a_low, b_high))


def dot_narrow(a, b_high, b_both):
    a_high, a_low = a
    both = dot(a_high, b_both)
    return both[:, :MODES] + (both[:, MODES:] + dot(a_low, b_high))


def pack_kernel(own_face, modes, basis, *outs):
    for direction, out in zip(slot_directions(), outs):
        first = pl.multiple_of(own_face[0, direction] * BLOCK, BLOCK)
        out[:BLOCK, :] = modes[pl.ds(first, BLOCK), :]
        out[BLOCK : BLOCK + MODES, :] = basis[:, :MODES]
        out[BLOCK + MODES :, :] = basis[:, MODES:]


def product_kernel(own_face, couplings, modes, stiffness, products, self_block, halves):
    high, low = split(modes[...])
    halves[:, :MODES] = high
    halves[:, MODES:] = low
    for slot, direction in enumerate(slot_directions()):
        first = pl.multiple_of(own_face[0, direction] * BLOCK, BLOCK)
        both = halves[pl.ds(first, BLOCK), :]
        products[slot] = dot_narrow(split(couplings[0, direction]), both[:, :MODES], both)
    scaled = modes[...].T * stiffness[...]
    both = halves[...]
    self_block[...] = dot_narrow(split(scaled), both[:, :MODES], both)


def term_kernel(present, products, self_block, basis, *refs):
    fetched, (blocks, terms, stack, others) = refs[:DIRS], refs[DIRS:]
    blocks[0, DIRS] = self_block[...]
    in_plane = [0]
    stack[:, :MODES] = self_block[...]
    others[:MODES, :] = basis[...]
    sides = {}
    left = split(basis[...].T)
    for slot, direction in enumerate(slot_directions()):
        kind, odd = EXCHANGES[slot]
        got = fetched[slot]
        far_high, far_low = split(got[:BLOCK, :])
        both = jnp.concatenate([far_high, far_low], axis=1)
        weight = present[0, direction].astype(F32)
        block = dot_narrow(split(products[slot].T), far_high, both) * weight
        blocks[0, direction] = block
        if kind == "group":
            far = jnp.concatenate([got[BLOCK : BLOCK + MODES, :], got[BLOCK + MODES :, :]], axis=1)
            half = dot_wide(split(block), split(far))
            term = dot_wide(left, split(half))
            terms[:, pl.ds(pl.multiple_of((direction - 4) * 2 * MODES2, MODES2), MODES2)] = term
        else:
            at = len(in_plane) * MODES
            in_plane.append(slot)
            stack[:, at : at + MODES] = block
            others[at : at + MODES, :MODES] = got[BLOCK : BLOCK + MODES, :]
            others[at : at + MODES, MODES:] = got[BLOCK + MODES :, :]
    half = dot_wide(split(stack[...]), split(others[...]))
    terms[:, MODES2 : 2 * MODES2] = dot_wide(left, split(half))


def sum_kernel(parts, out):
    total = parts[0]
    for other in range(1, SUBS):
        total = total + parts[other]
    for which in range(3):
        out[0, which] = total[:, which * MODES2 : (which + 1) * MODES2]


def body(couplings, mode_rows, coarse_basis, stiffness, own_face, neighbour_face, present):
    packed = pl.pallas_call(
        pack_kernel,
        out_shape=[jax.ShapeDtypeStruct((PACKED, MODES), F32)] * DIRS,
        in_specs=[SMEM, VMEM, VMEM],
        out_specs=[VMEM] * DIRS,
        name="pack",
    )(own_face, mode_rows, coarse_basis)
    fetched = [exchange(sent, kind, odd) for sent, (kind, odd) in zip(packed, EXCHANGES)]
    products, self_block = pl.pallas_call(
        product_kernel,
        out_shape=[
            jax.ShapeDtypeStruct((DIRS, BLOCK, MODES), F32),
            jax.ShapeDtypeStruct((MODES, MODES), F32),
        ],
        in_specs=[SMEM, VMEM, VMEM, VMEM],
        out_specs=[VMEM, VMEM],
        scratch_shapes=[pltpu.VMEM(mode_rows.shape[:1] + (2 * MODES,), BF16)],
        cost_estimate=pl.CostEstimate(flops=3 * 280_000_000, bytes_accessed=6_000_000, transcendentals=0),
        name="product",
    )(own_face, couplings, mode_rows, stiffness)
    blocks, terms = pl.pallas_call(
        term_kernel,
        out_shape=[
            jax.ShapeDtypeStruct((1, DIRS + 1, MODES, MODES), F32),
            jax.ShapeDtypeStruct((MODES2, 3 * MODES2), F32),
        ],
        in_specs=[SMEM] + [VMEM] * (3 + DIRS),
        out_specs=[VMEM, VMEM],
        scratch_shapes=[pltpu.VMEM((MODES, 5 * MODES), F32), pltpu.VMEM((5 * MODES, MODES2), F32)],
        cost_estimate=pl.CostEstimate(flops=3 * 200_000_000, bytes_accessed=4_000_000, transcendentals=0),
        name="term",
    )(present, products, self_block, coarse_basis, *fetched)
    rows = MODES2 // SUBS
    parts = lax.all_to_all(terms.reshape(SUBS, rows, 3 * MODES2), "sub", 0, 0)
    own_rows = pl.pallas_call(
        sum_kernel,
        out_shape=jax.ShapeDtypeStruct((1, 3, rows, MODES2), F32),
        in_specs=[VMEM],
        out_specs=VMEM,
        name="sum",
    )(parts)
    return (blocks, own_rows)


def solution(mesh):
    both = ("group", "sub")
    return jax.shard_map(
        body,
        mesh=mesh,
        in_specs=(
            P(both, None, None, None),
            P(both, None),
            P(both, None),
            P(both, None),
            P(both, None),
            P(both, None),
            P(both, None),
        ),
        out_specs=(P(both, None, None, None), P("group", None, "sub", None)),
        check_vma=False,
    )
```

```python
import jax
import jax.numpy as jnp
from jax import lax
from jax.experimental import pallas as pl
from jax.experimental.pallas import tpu as pltpu
from jax.sharding import PartitionSpec as P


DIRS = 6
SUB_ROW = 4
SUBS = 32
GROUPS = 16
BLOCK = 384
MODES = 128
MODES2 = 256
PACKED = BLOCK + MODES2
CHIPS = SUBS // 2
ROWS = MODES2 // SUBS

EXCHANGES = (("row", 0), ("row", 1), ("group", 0), ("group", 1), ("column", 1), ("column", 0))


F32 = jnp.float32
BF16 = jnp.bfloat16
SMEM = pl.BlockSpec(memory_space=pltpu.SMEM)
VMEM = pl.BlockSpec(memory_space=pltpu.VMEM)
HBM = pl.BlockSpec(memory_space=pltpu.HBM)


def swap_pairs(extent, odd):
    pairs = []
    for low in range(odd, extent - 1, 2):
        pairs += [(low, low + 1), (low + 1, low)]
    return pairs


def exchange(packed, kind, odd):
    if kind == "group":
        return lax.ppermute(packed, "group", swap_pairs(GROUPS, odd))
    pairs = []
    if kind == "row":
        for one, two in swap_pairs(SUBS // SUB_ROW, odd):
            pairs += [(one * SUB_ROW + c, two * SUB_ROW + c) for c in range(SUB_ROW)]
    else:
        for one, two in swap_pairs(SUB_ROW, odd):
            pairs += [(r * SUB_ROW + one, r * SUB_ROW + two) for r in range(SUBS // SUB_ROW)]
    return lax.ppermute(packed, "sub", pairs)


def slot_directions():
    sub, group = lax.axis_index("sub"), lax.axis_index("group")
    place = {
        "column": (lax.rem(sub, SUB_ROW), 0),
        "row": (lax.div(sub, SUB_ROW), 2),
        "group": (group, 4),
    }
    found = []
    for kind, odd in EXCHANGES:
        position, base = place[kind]
        found.append(base + 1 - lax.rem(position + odd, 2))
    return found


def split(x):
    high = x.astype(BF16)
    return high, (x - high.astype(F32)).astype(BF16)


def dot(a, b):
    return jnp.dot(a, b, preferred_element_type=F32)


def dot_wide(a, b):
    (a_high, a_low), (b_high, b_low) = a, b
    return dot(a_high, b_high) + (dot(a_high, b_low) + dot(a_low, b_high))


def dot_narrow(a, b_high, b_both):
    a_high, a_low = a
    both = dot(a_high, b_both)
    return both[:, :MODES] + (both[:, MODES:] + dot(a_low, b_high))


def pack_kernel(own_face, modes, basis, stiffness, *refs):
    outs, (near_modes, near_stiffness, faces, sems) = refs[:DIRS], refs[DIRS:]
    copies = [
        pltpu.make_async_copy(own_face, faces, sems.at[0]),
        pltpu.make_async_copy(modes, near_modes, sems.at[1]),
        pltpu.make_async_copy(stiffness, near_stiffness, sems.at[2]),
    ]
    for out in outs:
        for part in range(2):
            source = basis.at[:, part * MODES : (part + 1) * MODES]
            target = out.at[BLOCK + part * MODES : BLOCK + (part + 1) * MODES, :]
            copies.append(pltpu.make_async_copy(source, target, sems.at[len(copies)]))
    for copy in copies:
        copy.start()
    copies[0].wait()
    copies[1].wait()
    for direction, out in zip(slot_directions(), outs):
        first = pl.multiple_of(faces[0, direction] * BLOCK, BLOCK)
        out[:BLOCK, :] = near_modes[pl.ds(first, BLOCK), :]
    for copy in copies[2:]:
        copy.wait()


def self_kernel(modes, stiffness, self_block):
    high, low = split(modes[...])
    scaled = modes[...].T * stiffness[...]
    self_block[...] = dot_narrow(split(scaled), high, jnp.concatenate([high, low], axis=1))


def product_kernel(couplings, *refs):
    packed, (highs, lows) = refs[:DIRS], refs[DIRS:]
    for slot, direction in enumerate(slot_directions()):
        high, low = split(packed[slot][:BLOCK, :])
        both = jnp.concatenate([high, low], axis=1)
        product = dot_narrow(split(couplings[0, direction]), high, both)
        highs[slot], lows[slot] = split(product.T)


def half_kernel(present, highs, lows, self_block, own, *refs):
    fetched, (blocks, half, stack, others) = refs[:DIRS], refs[DIRS:]
    blocks[0, DIRS] = self_block[...]
    stack[:, :MODES] = self_block[...]
    others[:MODES, :MODES] = own[BLOCK : BLOCK + MODES, :]
    others[:MODES, MODES:] = own[BLOCK + MODES :, :]
    at = MODES
    for slot, direction in enumerate(slot_directions()):
        kind, _ = EXCHANGES[slot]
        got = fetched[slot]
        far_high, far_low = split(got[:BLOCK, :])
        both = jnp.concatenate([far_high, far_low], axis=1)
        weight = present[0, direction].astype(F32)
        block = dot_narrow((highs[slot], lows[slot]), far_high, both) * weight
        blocks[0, direction] = block
        if kind == "group":
            far = jnp.concatenate([got[BLOCK : BLOCK + MODES, :], got[BLOCK + MODES :, :]], axis=1)
            column = pl.multiple_of((direction - 4) * 2 * MODES2, MODES2)
            half[:, pl.ds(column, MODES2)] = dot_wide(split(block), split(far))
        else:
            stack[:, at : at + MODES] = block
            others[at : at + MODES, :MODES] = got[BLOCK : BLOCK + MODES, :]
            others[at : at + MODES, MODES:] = got[BLOCK + MODES :, :]
            at += MODES
    half[:, MODES2 : 2 * MODES2] = dot_wide(split(stack[...]), split(others[...]))


def term_kernel(own, partner, half, partner_half, near_blocks, terms, blocks, left, right, sem):
    copy = pltpu.make_async_copy(near_blocks, blocks, sem)
    copy.start()
    core = lax.rem(lax.axis_index("sub"), 2)
    for which, packed in enumerate((own, partner)):
        for part in range(2):
            piece = packed[BLOCK + part * MODES : BLOCK + (part + 1) * MODES, :]
            rows = piece.T.reshape(MODES // (2 * ROWS), 2, ROWS, MODES)
            chosen = jnp.where(core == 0, rows[:, 0], rows[:, 1]).reshape(MODES // 2, MODES)
            first = part * MODES // 2
            left[first : first + MODES // 2, which * MODES : (which + 1) * MODES] = chosen
    right[:MODES, :] = half[...]
    right[MODES:, :] = partner_half[...]
    terms[...] = dot_wide(split(left[...]), split(right[...])).reshape(terms.shape)
    copy.wait()


def sum_kernel(parts, out):
    total = parts[0]
    for other in range(1, CHIPS):
        total = total + parts[other]
    for which in range(3):
        out[0, which] = total[:, which * MODES2 : (which + 1) * MODES2]


def near(x):
    return pltpu.with_memory_space_constraint(x, pltpu.VMEM)


def far(x):
    return pltpu.with_memory_space_constraint(x, pltpu.HBM)


def call(kernel, ins, in_specs, outs, out_specs, scratch=(), flops=1_000_000):
    return pl.pallas_call(
        kernel,
        out_shape=outs,
        in_specs=in_specs,
        out_specs=out_specs,
        scratch_shapes=list(scratch),
        compiler_params=pltpu.CompilerParams(vmem_limit_bytes=16 << 20),
        cost_estimate=pl.CostEstimate(flops=flops, bytes_accessed=1_000_000, transcendentals=0),
    )(*ins)


def body(couplings, mode_rows, coarse_basis, stiffness, own_face, neighbour_face, present):
    *packed, modes, near_stiffness = call(
        pack_kernel,
        tuple(map(far, (own_face, mode_rows, coarse_basis, stiffness))),
        [HBM] * 4,
        [pltpu.VMEM((PACKED, MODES), F32)] * DIRS
        + [pltpu.VMEM(mode_rows.shape, F32), pltpu.VMEM(stiffness.shape, F32)],
        [VMEM] * (DIRS + 2),
        [pltpu.SMEM(own_face.shape, own_face.dtype), pltpu.SemaphoreType.DMA((3 + 2 * DIRS,))],
    )
    fetched = []
    for sent, (kind, odd) in zip(packed, EXCHANGES):
        fetched.append(near(exchange(sent, kind, odd)))
    (self_block,) = call(
        self_kernel,
        (modes, near_stiffness),
        [VMEM] * 2,
        [pltpu.VMEM((MODES, MODES), F32)],
        [VMEM],
        flops=4_000_000_000,
    )
    highs, lows = call(
        product_kernel,
        (near(couplings), *packed),
        [VMEM] * (1 + DIRS),
        [pltpu.VMEM((DIRS, MODES, BLOCK), BF16)] * 2,
        [VMEM] * 2,
        flops=800_000_000,
    )
    near_blocks, half = call(
        half_kernel,
        (present, highs, lows, self_block, packed[0], *fetched),
        [SMEM] + [VMEM] * (4 + DIRS),
        [pltpu.VMEM((1, DIRS + 1, MODES, MODES), F32), pltpu.VMEM((MODES, 3 * MODES2), F32)],
        [VMEM] * 2,
        [pltpu.VMEM((MODES, 5 * MODES), F32), pltpu.VMEM((5 * MODES, MODES2), F32)],
        flops=400_000_000,
    )
    partner_half = near(lax.ppermute(half, "sub", [(i, i ^ 1) for i in range(SUBS)]))
    terms, blocks = call(
        term_kernel,
        (packed[0], fetched[-1], half, partner_half, near_blocks),
        [VMEM] * 5,
        [
            pltpu.VMEM((CHIPS, ROWS, 3 * MODES2), F32),
            jax.ShapeDtypeStruct(near_blocks.shape, F32),
        ],
        [VMEM, HBM],
        [
            pltpu.VMEM((MODES, 2 * MODES), F32),
            pltpu.VMEM((2 * MODES, 3 * MODES2), F32),
            pltpu.SemaphoreType.DMA,
        ],
        flops=150_000_000,
    )
    chips = [[core + 2 * chip for chip in range(CHIPS)] for core in range(2)]
    parts = near(lax.all_to_all(terms, "sub", 0, 0, axis_index_groups=chips))
    (own_rows,) = call(
        sum_kernel, (parts,), [VMEM], [jax.ShapeDtypeStruct((1, 3, ROWS, MODES2), F32)], [VMEM]
    )
    return (blocks, own_rows)


def solution(mesh):
    both = ("group", "sub")
    return jax.shard_map(
        body,
        mesh=mesh,
        in_specs=(
            P(both, None, None, None),
            P(both, None),
            P(both, None),
            P(both, None),
            P(both, None),
            P(both, None),
            P(both, None),
        ),
        out_specs=(P(both, None, None, None), P("group", None, "sub", None)),
        check_vma=False,
    )
```

```python
import jax
import jax.numpy as jnp
from jax import lax
from jax.experimental import pallas as pl
from jax.experimental.pallas import tpu as pltpu
from jax.sharding import PartitionSpec as P


DIRS = 6
SUB_ROW = 4
SUBS = 32
GROUPS = 16
BLOCK = 384
MODES = 128
MODES2 = 256
PACKED = BLOCK + MODES2
CHIPS = SUBS // 2
ROWS = MODES2 // SUBS

EXCHANGES = (("row", 1), ("row", 0), ("group", 0), ("group", 1), ("column", 1), ("column", 0))
EARLY, LATE = (0, 2, 5), (1, 3, 4)


F32 = jnp.float32
BF16 = jnp.bfloat16
SMEM = pl.BlockSpec(memory_space=pltpu.SMEM)
VMEM = pl.BlockSpec(memory_space=pltpu.VMEM)
HBM = pl.BlockSpec(memory_space=pltpu.HBM)


def swap_pairs(extent, odd):
    pairs = []
    for low in range(odd, extent - 1, 2):
        pairs += [(low, low + 1), (low + 1, low)]
    return pairs


def exchange(packed, kind, odd):
    if kind == "group":
        return lax.ppermute(packed, "group", swap_pairs(GROUPS, odd))
    pairs = []
    if kind == "row":
        for one, two in swap_pairs(SUBS // SUB_ROW, odd):
            pairs += [(one * SUB_ROW + c, two * SUB_ROW + c) for c in range(SUB_ROW)]
    else:
        for one, two in swap_pairs(SUB_ROW, odd):
            pairs += [(r * SUB_ROW + one, r * SUB_ROW + two) for r in range(SUBS // SUB_ROW)]
    return lax.ppermute(packed, "sub", pairs)


def slot_directions():
    sub, group = lax.axis_index("sub"), lax.axis_index("group")
    place = {
        "column": (lax.rem(sub, SUB_ROW), 0),
        "row": (lax.div(sub, SUB_ROW), 2),
        "group": (group, 4),
    }
    found = []
    for kind, odd in EXCHANGES:
        position, base = place[kind]
        found.append(base + 1 - lax.rem(position + odd, 2))
    return found


def split(x):
    high = x.astype(BF16)
    return high, (x - high.astype(F32)).astype(BF16)


def dot(a, b):
    return jnp.dot(a, b, preferred_element_type=F32)


def dot_wide(a, b):
    (a_high, a_low), (b_high, b_low) = a, b
    return dot(a_high, b_high) + (dot(a_high, b_low) + dot(a_low, b_high))


def dot_narrow(a, b_high, b_both):
    a_high, a_low = a
    both = dot(a_high, b_both)
    return both[:, :MODES] + (both[:, MODES:] + dot(a_low, b_high))


def pack_kernel(own_face, modes, basis, stiffness, *refs):
    outs, (near_modes, near_stiffness, faces, sems) = refs[:DIRS], refs[DIRS:]
    copies = [
        pltpu.make_async_copy(own_face, faces, sems.at[0]),
        pltpu.make_async_copy(modes, near_modes, sems.at[1]),
        pltpu.make_async_copy(stiffness, near_stiffness, sems.at[2]),
    ]
    for out in outs:
        for part in range(2):
            source = basis.at[:, part * MODES : (part + 1) * MODES]
            target = out.at[BLOCK + part * MODES : BLOCK + (part + 1) * MODES, :]
            copies.append(pltpu.make_async_copy(source, target, sems.at[len(copies)]))
    for copy in copies:
        copy.start()
    copies[0].wait()
    copies[1].wait()
    for direction, out in zip(slot_directions(), outs):
        first = pl.multiple_of(faces[0, direction] * BLOCK, BLOCK)
        out[:BLOCK, :] = near_modes[pl.ds(first, BLOCK), :]
    for copy in copies[2:]:
        copy.wait()


def self_kernel(modes, stiffness, self_block):
    high, low = split(modes[...])
    scaled = modes[...].T * stiffness[...]
    self_block[...] = dot_narrow(split(scaled), high, jnp.concatenate([high, low], axis=1))


def product_kernel(couplings, *refs):
    packed, (highs, lows) = refs[:DIRS], refs[DIRS:]
    for slot, direction in enumerate(slot_directions()):
        high, low = split(packed[slot][:BLOCK, :])
        both = jnp.concatenate([high, low], axis=1)
        product = dot_narrow(split(couplings[0, direction]), high, both)
        highs[slot], lows[slot] = split(product.T)


def coarse_block(present, highs, lows, got, slot, direction):
    far_high, far_low = split(got[:BLOCK, :])
    both = jnp.concatenate([far_high, far_low], axis=1)
    weight = present[0, direction].astype(F32)
    return dot_narrow((highs[slot], lows[slot]), far_high, both) * weight


def half_terms(present, highs, lows, slots, fetched, blocks, stack, others, at):
    directions = slot_directions()
    for place, (slot, got) in enumerate(zip(slots, fetched)):
        block = coarse_block(present, highs, lows, got, slot, directions[slot])
        blocks[place] = block
        low, high = got[BLOCK : BLOCK + MODES, :], got[BLOCK + MODES :, :]
        if EXCHANGES[slot][0] == "group":
            outer = dot_wide(split(block), split(jnp.concatenate([low, high], axis=1)))
        else:
            stack[:, at : at + MODES] = block
            others[at : at + MODES, :MODES] = low
            others[at : at + MODES, MODES:] = high
            at += MODES
    return outer, dot_wide(split(stack[...]), split(others[...]))


def early_kernel(present, highs, lows, self_block, own, *refs):
    fetched, (blocks, outer, within, stack, others) = refs[: len(EARLY)], refs[len(EARLY) :]
    stack[:, :MODES] = self_block[...]
    others[:MODES, :MODES] = own[BLOCK : BLOCK + MODES, :]
    others[:MODES, MODES:] = own[BLOCK + MODES :, :]
    outer[...], within[...] = half_terms(
        present, highs, lows, EARLY, fetched, blocks, stack, others, MODES
    )


def late_kernel(present, highs, lows, early_outer, early_within, *refs):
    fetched, (blocks, half, stack, others) = refs[: len(LATE)], refs[len(LATE) :]
    outer, within = half_terms(present, highs, lows, LATE, fetched, blocks, stack, others, 0)
    half[:, MODES2 : 2 * MODES2] = within + early_within[...]
    for slots, part in ((EARLY, early_outer[...]), (LATE, outer)):
        (slot,) = [slot for slot in slots if EXCHANGES[slot][0] == "group"]
        column = pl.multiple_of((slot_directions()[slot] - 4) * 2 * MODES2, MODES2)
        half[:, pl.ds(column, MODES2)] = part


def left_kernel(own, partner, half, self_block, early, late, left, terms, blocks, stack, sems):
    copies = [pltpu.make_async_copy(self_block, blocks.at[0, DIRS], sems.at[DIRS])]
    for slots, near_blocks in ((EARLY, early), (LATE, late)):
        for place, slot in enumerate(slots):
            target = blocks.at[0, slot_directions()[slot]]
            copies.append(pltpu.make_async_copy(near_blocks.at[place], target, sems.at[slot]))
    for copy in copies:
        copy.start()
    core = lax.rem(lax.axis_index("sub"), 2)
    for which, packed in enumerate((own, partner)):
        for part in range(2):
            piece = packed[BLOCK + part * MODES : BLOCK + (part + 1) * MODES, :]
            rows = piece.T.reshape(MODES // (2 * ROWS), 2, ROWS, MODES)
            chosen = jnp.where(core == 0, rows[:, 0], rows[:, 1]).reshape(MODES // 2, MODES)
            first = part * MODES // 2
            stack[which, first : first + MODES // 2, :] = chosen
    left[0], left[1] = split(stack[1])
    terms[...] = dot_wide(split(stack[0]), split(half[...]))
    for copy in copies:
        copy.wait()


def term_kernel(left, partner_half, own_terms, terms):
    product = dot_wide((left[0], left[1]), split(partner_half[...]))
    terms[...] = (own_terms[...] + product).reshape(terms.shape)


def sum_kernel(parts, out):
    total = parts[0]
    for other in range(1, CHIPS):
        total = total + parts[other]
    for which in range(3):
        out[0, which] = total[:, which * MODES2 : (which + 1) * MODES2]


def near(x):
    return pltpu.with_memory_space_constraint(x, pltpu.VMEM)


def far(x):
    return pltpu.with_memory_space_constraint(x, pltpu.HBM)


def call(kernel, ins, in_specs, outs, out_specs, scratch=(), flops=1_000_000):
    return pl.pallas_call(
        kernel,
        out_shape=outs,
        in_specs=in_specs,
        out_specs=out_specs,
        scratch_shapes=list(scratch),
        compiler_params=pltpu.CompilerParams(vmem_limit_bytes=16 << 20),
        cost_estimate=pl.CostEstimate(flops=flops, bytes_accessed=1_000_000, transcendentals=0),
    )(*ins)


def body(couplings, mode_rows, coarse_basis, stiffness, own_face, neighbour_face, present):
    *packed, modes, near_stiffness = call(
        pack_kernel,
        tuple(map(far, (own_face, mode_rows, coarse_basis, stiffness))),
        [HBM] * 4,
        [pltpu.VMEM((PACKED, MODES), F32)] * DIRS
        + [pltpu.VMEM(mode_rows.shape, F32), pltpu.VMEM(stiffness.shape, F32)],
        [VMEM] * (DIRS + 2),
        [pltpu.SMEM(own_face.shape, own_face.dtype), pltpu.SemaphoreType.DMA((3 + 2 * DIRS,))],
    )
    fetched = []
    for sent, (kind, odd) in zip(packed, EXCHANGES):
        fetched.append(near(exchange(sent, kind, odd)))
    (self_block,) = call(
        self_kernel,
        (modes, near_stiffness),
        [VMEM] * 2,
        [pltpu.VMEM((MODES, MODES), F32)],
        [VMEM],
        flops=4_000_000_000,
    )
    highs, lows = call(
        product_kernel,
        (near(couplings), *packed),
        [VMEM] * (1 + DIRS),
        [pltpu.VMEM((DIRS, MODES, BLOCK), BF16)] * 2,
        [VMEM] * 2,
        flops=800_000_000,
    )
    block_shape, half_shape = (MODES, MODES), (MODES, MODES2)
    early_blocks, early_outer, early_within = call(
        early_kernel,
        (present, highs, lows, self_block, packed[0], *[fetched[slot] for slot in EARLY]),
        [SMEM] + [VMEM] * (4 + len(EARLY)),
        [pltpu.VMEM((len(EARLY), *block_shape), F32)] + [pltpu.VMEM(half_shape, F32)] * 2,
        [VMEM] * 3,
        [pltpu.VMEM((MODES, 3 * MODES), F32), pltpu.VMEM((3 * MODES, MODES2), F32)],
        flops=200_000_000,
    )
    late_blocks, half = call(
        late_kernel,
        (present, highs, lows, early_outer, early_within, *[fetched[slot] for slot in LATE]),
        [SMEM] + [VMEM] * (4 + len(LATE)),
        [pltpu.VMEM((len(LATE), *block_shape), F32), pltpu.VMEM((MODES, 3 * MODES2), F32)],
        [VMEM] * 2,
        [pltpu.VMEM((MODES, 2 * MODES), F32), pltpu.VMEM((2 * MODES, MODES2), F32)],
        flops=200_000_000,
    )
    partner_half = near(lax.ppermute(half, "sub", [(i, i ^ 1) for i in range(SUBS)]))
    partner = fetched[EXCHANGES.index(("column", 0))]
    left, own_terms, blocks = call(
        left_kernel,
        (packed[0], partner, half, self_block, early_blocks, late_blocks),
        [VMEM] * 6,
        [
            pltpu.VMEM((2, MODES, MODES), BF16),
            pltpu.VMEM((MODES, 3 * MODES2), F32),
            jax.ShapeDtypeStruct((1, DIRS + 1, MODES, MODES), F32),
        ],
        [VMEM, VMEM, HBM],
        [pltpu.VMEM((2, MODES, MODES), F32), pltpu.SemaphoreType.DMA((DIRS + 1,))],
        flops=150_000_000,
    )
    (terms,) = call(
        term_kernel,
        (left, partner_half, own_terms),
        [VMEM] * 3,
        [pltpu.VMEM((CHIPS, ROWS, 3 * MODES2), F32)],
        [VMEM],
        flops=150_000_000,
    )
    chips = [[core + 2 * chip for chip in range(CHIPS)] for core in range(2)]
    parts = near(lax.all_to_all(terms, "sub", 0, 0, axis_index_groups=chips))
    (own_rows,) = call(
        sum_kernel, (parts,), [VMEM], [jax.ShapeDtypeStruct((1, 3, ROWS, MODES2), F32)], [VMEM]
    )
    return (blocks, own_rows)


def solution(mesh):
    both = ("group", "sub")
    return jax.shard_map(
        body,
        mesh=mesh,
        in_specs=(
            P(both, None, None, None),
            P(both, None),
            P(both, None),
            P(both, None),
            P(both, None),
            P(both, None),
            P(both, None),
        ),
        out_specs=(P(both, None, None, None), P("group", None, "sub", None)),
        check_vma=False,
    )
```

```python
import jax
import jax.numpy as jnp
from jax import lax
from jax.experimental import pallas as pl
from jax.experimental.pallas import tpu as pltpu
from jax.sharding import PartitionSpec as P


DIRS = 6
SUB_ROW = 4
SUBS = 32
GROUPS = 16
BLOCK = 384
MODES = 128
MODES2 = 256
PACKED = BLOCK + MODES2
CHIPS = SUBS // 2
ROWS = MODES2 // SUBS

EXCHANGES = (("row", 1), ("row", 0), ("group", 0), ("group", 1), ("column", 1), ("column", 0))
EARLY, LATE = (0, 2, 5), (1, 3, 4)


F32 = jnp.float32
BF16 = jnp.bfloat16
SMEM = pl.BlockSpec(memory_space=pltpu.SMEM)
VMEM = pl.BlockSpec(memory_space=pltpu.VMEM)
HBM = pl.BlockSpec(memory_space=pltpu.HBM)


def swap_pairs(extent, odd):
    pairs = []
    for low in range(odd, extent - 1, 2):
        pairs += [(low, low + 1), (low + 1, low)]
    return pairs


def exchange(packed, kind, odd):
    if kind == "group":
        return lax.ppermute(packed, "group", swap_pairs(GROUPS, odd))
    pairs = []
    if kind == "row":
        for one, two in swap_pairs(SUBS // SUB_ROW, odd):
            pairs += [(one * SUB_ROW + c, two * SUB_ROW + c) for c in range(SUB_ROW)]
    else:
        for one, two in swap_pairs(SUB_ROW, odd):
            pairs += [(r * SUB_ROW + one, r * SUB_ROW + two) for r in range(SUBS // SUB_ROW)]
    return lax.ppermute(packed, "sub", pairs)


def slot_directions():
    sub, group = lax.axis_index("sub"), lax.axis_index("group")
    place = {
        "column": (lax.rem(sub, SUB_ROW), 0),
        "row": (lax.div(sub, SUB_ROW), 2),
        "group": (group, 4),
    }
    found = []
    for kind, odd in EXCHANGES:
        position, base = place[kind]
        found.append(base + 1 - lax.rem(position + odd, 2))
    return found


def split(x):
    high = x.astype(BF16)
    return high, (x - high.astype(F32)).astype(BF16)


def dot(a, b):
    return jnp.dot(a, b, preferred_element_type=F32)


def dot_wide(a, b):
    (a_high, a_low), (b_high, b_low) = a, b
    count = a_high.shape[0]
    tall = dot(jnp.concatenate([a_high, a_low], axis=0), b_high)
    return tall[:count] + (tall[count:] + dot(a_high, b_low))


def dot_stacked(a, b_both):
    a_high, a_low = a
    count = a_high.shape[0]
    tall = dot(jnp.concatenate([a_high, a_low], axis=0), b_both)
    return tall[:count, :MODES] + (tall[:count, MODES:] + tall[count:, :MODES])


def dot_narrow(a, b_high, b_both):
    a_high, a_low = a
    both = dot(a_high, b_both)
    return both[:, :MODES] + (both[:, MODES:] + dot(a_low, b_high))


def pack_kernel(own_face, modes, basis, stiffness, *refs):
    outs, (near_modes, near_stiffness, faces, sems) = refs[:DIRS], refs[DIRS:]
    copies = [
        pltpu.make_async_copy(own_face, faces, sems.at[0]),
        pltpu.make_async_copy(modes, near_modes, sems.at[1]),
        pltpu.make_async_copy(stiffness, near_stiffness, sems.at[2]),
    ]
    for out in outs:
        for part in range(2):
            source = basis.at[:, part * MODES : (part + 1) * MODES]
            target = out.at[BLOCK + part * MODES : BLOCK + (part + 1) * MODES, :]
            copies.append(pltpu.make_async_copy(source, target, sems.at[len(copies)]))
    for copy in copies:
        copy.start()
    copies[0].wait()
    copies[1].wait()
    for direction, out in zip(slot_directions(), outs):
        first = pl.multiple_of(faces[0, direction] * BLOCK, BLOCK)
        out[:BLOCK, :] = near_modes[pl.ds(first, BLOCK), :]
    for copy in copies[2:]:
        copy.wait()


def marker_kernel(marker):
    marker[...] = jnp.zeros_like(marker)


def product_kernel(couplings, modes, stiffness, marker, *refs):
    packed, (highs, lows, self_block) = refs[:DIRS], refs[DIRS:]
    high, low = split(modes[...])
    scaled = modes[...].T * stiffness[...]
    self_block[...] = dot_narrow(split(scaled), high, jnp.concatenate([high, low], axis=1))
    for slot, direction in enumerate(slot_directions()):
        high, low = split(packed[slot][:BLOCK, :])
        both = jnp.concatenate([high, low], axis=1)
        product = dot_narrow(split(couplings[0, direction]), high, both)
        highs[slot], lows[slot] = split(product.T)


def coarse_block(present, highs, lows, got, slot, direction):
    far_high, far_low = split(got[:BLOCK, :])
    both = jnp.concatenate([far_high, far_low], axis=1)
    weight = present[0, direction].astype(F32)
    return dot_stacked((highs[slot], lows[slot]), both) * weight


def half_terms(present, highs, lows, slots, fetched, blocks, stack, others, at):
    directions = slot_directions()
    for place, (slot, got) in enumerate(zip(slots, fetched)):
        block = coarse_block(present, highs, lows, got, slot, directions[slot])
        blocks[place] = block
        low, high = got[BLOCK : BLOCK + MODES, :], got[BLOCK + MODES :, :]
        if EXCHANGES[slot][0] == "group":
            outer = dot_wide(split(block), split(jnp.concatenate([low, high], axis=1)))
        else:
            stack[:, at : at + MODES] = block
            others[at : at + MODES, :MODES] = low
            others[at : at + MODES, MODES:] = high
            at += MODES
    return outer, dot_wide(split(stack[...]), split(others[...]))


def early_kernel(present, highs, lows, self_block, own, *refs):
    fetched, (blocks, outer, within, stack, others) = refs[: len(EARLY)], refs[len(EARLY) :]
    stack[:, :MODES] = self_block[...]
    others[:MODES, :MODES] = own[BLOCK : BLOCK + MODES, :]
    others[:MODES, MODES:] = own[BLOCK + MODES :, :]
    outer[...], within[...] = half_terms(
        present, highs, lows, EARLY, fetched, blocks, stack, others, MODES
    )


def late_kernel(present, highs, lows, early_outer, early_within, *refs):
    fetched, (blocks, half, stack, others) = refs[: len(LATE)], refs[len(LATE) :]
    outer, within = half_terms(present, highs, lows, LATE, fetched, blocks, stack, others, 0)
    half[:, MODES2 : 2 * MODES2] = within + early_within[...]
    for slots, part in ((EARLY, early_outer[...]), (LATE, outer)):
        (slot,) = [slot for slot in slots if EXCHANGES[slot][0] == "group"]
        column = pl.multiple_of((slot_directions()[slot] - 4) * 2 * MODES2, MODES2)
        half[:, pl.ds(column, MODES2)] = part


def left_kernel(own, partner, half, self_block, early, late, left, terms, blocks, stack, sems):
    copies = [pltpu.make_async_copy(self_block, blocks.at[0, DIRS], sems.at[DIRS])]
    for slots, near_blocks in ((EARLY, early), (LATE, late)):
        for place, slot in enumerate(slots):
            target = blocks.at[0, slot_directions()[slot]]
            copies.append(pltpu.make_async_copy(near_blocks.at[place], target, sems.at[slot]))
    for copy in copies:
        copy.start()
    core = lax.rem(lax.axis_index("sub"), 2)
    for which, packed in enumerate((own, partner)):
        for part in range(2):
            piece = packed[BLOCK + part * MODES : BLOCK + (part + 1) * MODES, :]
            rows = piece.T.reshape(MODES // (2 * ROWS), 2, ROWS, MODES)
            chosen = jnp.where(core == 0, rows[:, 0], rows[:, 1]).reshape(MODES // 2, MODES)
            first = part * MODES // 2
            stack[which, first : first + MODES // 2, :] = chosen
    left[0], left[1] = split(stack[1])
    terms[...] = dot_wide(split(stack[0]), split(half[...]))
    for copy in copies:
        copy.wait()


def term_kernel(left, partner_half, own_terms, terms):
    product = dot_wide((left[0], left[1]), split(partner_half[...]))
    terms[...] = (own_terms[...] + product).reshape(terms.shape)


def sum_kernel(parts, out):
    total = parts[0]
    for other in range(1, CHIPS):
        total = total + parts[other]
    for which in range(3):
        out[0, which] = total[:, which * MODES2 : (which + 1) * MODES2]


def near(x):
    return pltpu.with_memory_space_constraint(x, pltpu.VMEM)


def far(x):
    return pltpu.with_memory_space_constraint(x, pltpu.HBM)


def call(kernel, ins, in_specs, outs, out_specs, scratch=(), flops=1_000_000):
    return pl.pallas_call(
        kernel,
        out_shape=outs,
        in_specs=in_specs,
        out_specs=out_specs,
        scratch_shapes=list(scratch),
        compiler_params=pltpu.CompilerParams(vmem_limit_bytes=16 << 20),
        cost_estimate=pl.CostEstimate(flops=flops, bytes_accessed=1_000_000, transcendentals=0),
    )(*ins)


def body(couplings, mode_rows, coarse_basis, stiffness, own_face, neighbour_face, present):
    *packed, modes, near_stiffness = call(
        pack_kernel,
        tuple(map(far, (own_face, mode_rows, coarse_basis, stiffness))),
        [HBM] * 4,
        [pltpu.VMEM((PACKED, MODES), F32)] * DIRS
        + [pltpu.VMEM(mode_rows.shape, F32), pltpu.VMEM(stiffness.shape, F32)],
        [VMEM] * (DIRS + 2),
        [pltpu.SMEM(own_face.shape, own_face.dtype), pltpu.SemaphoreType.DMA((3 + 2 * DIRS,))],
    )
    fetched = []
    for sent, (kind, odd) in zip(packed, EXCHANGES):
        fetched.append(near(exchange(sent, kind, odd)))
    (marker,) = call(
        marker_kernel, (), [], [pltpu.VMEM((8, MODES), F32)], [VMEM], flops=4_000_000_000
    )
    highs, lows, self_block = call(
        product_kernel,
        (near(couplings), modes, near_stiffness, marker, *packed),
        [VMEM] * (4 + DIRS),
        [pltpu.VMEM((DIRS, MODES, BLOCK), BF16)] * 2 + [pltpu.VMEM((MODES, MODES), F32)],
        [VMEM] * 3,
        flops=800_000_000,
    )
    block_shape, half_shape = (MODES, MODES), (MODES, MODES2)
    early_blocks, early_outer, early_within = call(
        early_kernel,
        (present, highs, lows, self_block, packed[0], *[fetched[slot] for slot in EARLY]),
        [SMEM] + [VMEM] * (4 + len(EARLY)),
        [pltpu.VMEM((len(EARLY), *block_shape), F32)] + [pltpu.VMEM(half_shape, F32)] * 2,
        [VMEM] * 3,
        [
            pltpu.VMEM((MODES, len(EARLY) * MODES), F32),
            pltpu.VMEM((len(EARLY) * MODES, MODES2), F32),
        ],
        flops=200_000_000,
    )
    late_blocks, half = call(
        late_kernel,
        (present, highs, lows, early_outer, early_within, *[fetched[slot] for slot in LATE]),
        [SMEM] + [VMEM] * (4 + len(LATE)),
        [pltpu.VMEM((len(LATE), *block_shape), F32), pltpu.VMEM((MODES, 3 * MODES2), F32)],
        [VMEM] * 2,
        [
            pltpu.VMEM((MODES, (len(LATE) - 1) * MODES), F32),
            pltpu.VMEM(((len(LATE) - 1) * MODES, MODES2), F32),
        ],
        flops=200_000_000,
    )
    partner_half = near(lax.ppermute(half, "sub", [(i, i ^ 1) for i in range(SUBS)]))
    partner = fetched[EXCHANGES.index(("column", 0))]
    left, own_terms, blocks = call(
        left_kernel,
        (packed[0], partner, half, self_block, early_blocks, late_blocks),
        [VMEM] * 6,
        [
            pltpu.VMEM((2, MODES, MODES), BF16),
            pltpu.VMEM((MODES, 3 * MODES2), F32),
            jax.ShapeDtypeStruct((1, DIRS + 1, MODES, MODES), F32),
        ],
        [VMEM, VMEM, HBM],
        [pltpu.VMEM((2, MODES, MODES), F32), pltpu.SemaphoreType.DMA((DIRS + 1,))],
        flops=150_000_000,
    )
    (terms,) = call(
        term_kernel,
        (left, partner_half, own_terms),
        [VMEM] * 3,
        [pltpu.VMEM((CHIPS, ROWS, 3 * MODES2), F32)],
        [VMEM],
        flops=150_000_000,
    )
    chips = [[core + 2 * chip for chip in range(CHIPS)] for core in range(2)]
    parts = near(lax.all_to_all(terms, "sub", 0, 0, axis_index_groups=chips))
    (own_rows,) = call(
        sum_kernel, (parts,), [VMEM], [jax.ShapeDtypeStruct((1, 3, ROWS, MODES2), F32)], [VMEM]
    )
    return (blocks, own_rows)


def solution(mesh):
    both = ("group", "sub")
    return jax.shard_map(
        body,
        mesh=mesh,
        in_specs=(
            P(both, None, None, None),
            P(both, None),
            P(both, None),
            P(both, None),
            P(both, None),
            P(both, None),
            P(both, None),
        ),
        out_specs=(P(both, None, None, None), P("group", None, "sub", None)),
        check_vma=False,
    )
```

```python
import jax
import jax.numpy as jnp
from jax import lax
from jax.experimental import pallas as pl
from jax.experimental.pallas import tpu as pltpu
from jax.sharding import PartitionSpec as P


DIRS = 6
SUB_ROW = 4
SUBS = 32
GROUPS = 16
BLOCK = 384
MODES = 128
MODES2 = 256
PACKED = BLOCK + MODES2
CHIPS = SUBS // 2
ROWS = MODES2 // SUBS

EXCHANGES = (("row", 1), ("row", 0), ("group", 0), ("group", 1), ("column", 1), ("column", 0))
EARLY, LATE = (0, 2, 5), (1, 3, 4)


F32 = jnp.float32
BF16 = jnp.bfloat16
SMEM = pl.BlockSpec(memory_space=pltpu.SMEM)
VMEM = pl.BlockSpec(memory_space=pltpu.VMEM)
HBM = pl.BlockSpec(memory_space=pltpu.HBM)


def swap_pairs(extent, odd):
    pairs = []
    for low in range(odd, extent - 1, 2):
        pairs += [(low, low + 1), (low + 1, low)]
    return pairs


def exchange(packed, kind, odd):
    if kind == "group":
        return lax.ppermute(packed, "group", swap_pairs(GROUPS, odd))
    pairs = []
    if kind == "row":
        for one, two in swap_pairs(SUBS // SUB_ROW, odd):
            pairs += [(one * SUB_ROW + c, two * SUB_ROW + c) for c in range(SUB_ROW)]
    else:
        for one, two in swap_pairs(SUB_ROW, odd):
            pairs += [(r * SUB_ROW + one, r * SUB_ROW + two) for r in range(SUBS // SUB_ROW)]
    return lax.ppermute(packed, "sub", pairs)


def slot_directions():
    sub, group = lax.axis_index("sub"), lax.axis_index("group")
    place = {
        "column": (lax.rem(sub, SUB_ROW), 0),
        "row": (lax.div(sub, SUB_ROW), 2),
        "group": (group, 4),
    }
    found = []
    for kind, odd in EXCHANGES:
        position, base = place[kind]
        found.append(base + 1 - lax.rem(position + odd, 2))
    return found


def split(x):
    high = x.astype(BF16)
    return high, (x - high.astype(F32)).astype(BF16)


def dot(a, b):
    return jnp.dot(a, b, preferred_element_type=F32)


def dot_wide(a, b):
    (a_high, a_low), (b_high, b_low) = a, b
    count = a_high.shape[0]
    tall = dot(jnp.concatenate([a_high, a_low], axis=0), b_high)
    return tall[:count] + (tall[count:] + dot(a_high, b_low))


def dot_stacked(a, b_both):
    a_high, a_low = a
    count = a_high.shape[0]
    tall = dot(jnp.concatenate([a_high, a_low], axis=0), b_both)
    return tall[:count, :MODES] + (tall[:count, MODES:] + tall[count:, :MODES])


def dot_narrow(a, b_high, b_both):
    a_high, a_low = a
    both = dot(a_high, b_both)
    return both[:, :MODES] + (both[:, MODES:] + dot(a_low, b_high))


def pack_kernel(own_face, modes, basis, stiffness, *refs):
    outs, (near_modes, near_stiffness, faces, sems) = refs[:DIRS], refs[DIRS:]
    copies = [
        pltpu.make_async_copy(own_face, faces, sems.at[0]),
        pltpu.make_async_copy(modes, near_modes, sems.at[1]),
        pltpu.make_async_copy(stiffness, near_stiffness, sems.at[2]),
    ]
    for part in range(2):
        source = basis.at[:, part * MODES : (part + 1) * MODES]
        target = outs[0].at[BLOCK + part * MODES : BLOCK + (part + 1) * MODES, :]
        copies.append(pltpu.make_async_copy(source, target, sems.at[len(copies)]))
    for copy in copies:
        copy.start()
    for copy in copies[2:]:
        copy.wait()
    for out in outs[1:]:
        out[BLOCK:, :] = outs[0][BLOCK:, :]
    copies[0].wait()
    copies[1].wait()
    for direction, out in zip(slot_directions(), outs):
        first = pl.multiple_of(faces[0, direction] * BLOCK, BLOCK)
        out[:BLOCK, :] = near_modes[pl.ds(first, BLOCK), :]


def marker_kernel(marker):
    marker[...] = jnp.zeros_like(marker)


def product_kernel(couplings, modes, stiffness, marker, *refs):
    packed, (highs, lows, self_block) = refs[:DIRS], refs[DIRS:]
    high, low = split(modes[...])
    scaled = modes[...].T * stiffness[...]
    self_block[...] = dot_narrow(split(scaled), high, jnp.concatenate([high, low], axis=1))
    for slot, direction in enumerate(slot_directions()):
        high, low = split(packed[slot][:BLOCK, :])
        both = jnp.concatenate([high, low], axis=1)
        product = dot_narrow(split(couplings[0, direction]), high, both)
        highs[slot], lows[slot] = split(product.T)


def coarse_block(present, highs, lows, got, slot, direction):
    far_high, far_low = split(got[:BLOCK, :])
    both = jnp.concatenate([far_high, far_low], axis=1)
    weight = present[0, direction].astype(F32)
    return dot_stacked((highs[slot], lows[slot]), both) * weight


def half_terms(present, highs, lows, slots, fetched, blocks, stack, others, at):
    directions = slot_directions()
    for place, (slot, got) in enumerate(zip(slots, fetched)):
        block = coarse_block(present, highs, lows, got, slot, directions[slot])
        blocks[place] = block
        low, high = got[BLOCK : BLOCK + MODES, :], got[BLOCK + MODES :, :]
        if EXCHANGES[slot][0] == "group":
            outer = dot_wide(split(block), split(jnp.concatenate([low, high], axis=1)))
        else:
            stack[:, at : at + MODES] = block
            others[at : at + MODES, :MODES] = low
            others[at : at + MODES, MODES:] = high
            at += MODES
    return outer, dot_wide(split(stack[...]), split(others[...]))


def early_kernel(present, highs, lows, self_block, own, *refs):
    fetched, (blocks, outer, within, stack, others) = refs[: len(EARLY)], refs[len(EARLY) :]
    stack[:, :MODES] = self_block[...]
    others[:MODES, :MODES] = own[BLOCK : BLOCK + MODES, :]
    others[:MODES, MODES:] = own[BLOCK + MODES :, :]
    outer[...], within[...] = half_terms(
        present, highs, lows, EARLY, fetched, blocks, stack, others, MODES
    )


def late_kernel(present, highs, lows, early_outer, early_within, *refs):
    fetched, (blocks, half, stack, others) = refs[: len(LATE)], refs[len(LATE) :]
    outer, within = half_terms(present, highs, lows, LATE, fetched, blocks, stack, others, 0)
    half[:, MODES2 : 2 * MODES2] = within + early_within[...]
    for slots, part in ((EARLY, early_outer[...]), (LATE, outer)):
        (slot,) = [slot for slot in slots if EXCHANGES[slot][0] == "group"]
        column = pl.multiple_of((slot_directions()[slot] - 4) * 2 * MODES2, MODES2)
        half[:, pl.ds(column, MODES2)] = part


def left_kernel(own, partner, half, self_block, early, late, left, terms, blocks, stack, sems):
    copies = [pltpu.make_async_copy(self_block, blocks.at[0, DIRS], sems.at[DIRS])]
    for slots, near_blocks in ((EARLY, early), (LATE, late)):
        for place, slot in enumerate(slots):
            target = blocks.at[0, slot_directions()[slot]]
            copies.append(pltpu.make_async_copy(near_blocks.at[place], target, sems.at[slot]))
    for copy in copies:
        copy.start()
    core = lax.rem(lax.axis_index("sub"), 2)
    for which, packed in enumerate((own, partner)):
        for part in range(2):
            piece = packed[BLOCK + part * MODES : BLOCK + (part + 1) * MODES, :]
            rows = piece.T.reshape(MODES // (2 * ROWS), 2, ROWS, MODES)
            chosen = jnp.where(core == 0, rows[:, 0], rows[:, 1]).reshape(MODES // 2, MODES)
            first = part * MODES // 2
            stack[which, first : first + MODES // 2, :] = chosen
    left[0], left[1] = split(stack[1])
    terms[...] = dot_wide(split(stack[0]), split(half[...]))
    for copy in copies:
        copy.wait()


def term_kernel(left, partner_half, own_terms, terms):
    product = dot_wide((left[0], left[1]), split(partner_half[...]))
    terms[...] = (own_terms[...] + product).reshape(terms.shape)


def sum_kernel(parts, out):
    total = parts[0]
    for other in range(1, CHIPS):
        total = total + parts[other]
    for which in range(3):
        out[0, which] = total[:, which * MODES2 : (which + 1) * MODES2]


def near(x):
    return pltpu.with_memory_space_constraint(x, pltpu.VMEM)


def far(x):
    return pltpu.with_memory_space_constraint(x, pltpu.HBM)


def call(kernel, ins, in_specs, outs, out_specs, scratch=(), flops=1_000_000):
    return pl.pallas_call(
        kernel,
        out_shape=outs,
        in_specs=in_specs,
        out_specs=out_specs,
        scratch_shapes=list(scratch),
        compiler_params=pltpu.CompilerParams(vmem_limit_bytes=16 << 20),
        cost_estimate=pl.CostEstimate(flops=flops, bytes_accessed=1_000_000, transcendentals=0),
    )(*ins)


def body(couplings, mode_rows, coarse_basis, stiffness, own_face, neighbour_face, present):
    *packed, modes, near_stiffness = call(
        pack_kernel,
        tuple(map(far, (own_face, mode_rows, coarse_basis, stiffness))),
        [HBM] * 4,
        [pltpu.VMEM((PACKED, MODES), F32)] * DIRS
        + [pltpu.VMEM(mode_rows.shape, F32), pltpu.VMEM(stiffness.shape, F32)],
        [VMEM] * (DIRS + 2),
        [pltpu.SMEM(own_face.shape, own_face.dtype), pltpu.SemaphoreType.DMA((5,))],
    )
    fetched = []
    for sent, (kind, odd) in zip(packed, EXCHANGES):
        fetched.append(near(exchange(sent, kind, odd)))
    (marker,) = call(
        marker_kernel, (), [], [pltpu.VMEM((8, MODES), F32)], [VMEM], flops=4_000_000_000
    )
    highs, lows, self_block = call(
        product_kernel,
        (near(couplings), modes, near_stiffness, marker, *packed),
        [VMEM] * (4 + DIRS),
        [pltpu.VMEM((DIRS, MODES, BLOCK), BF16)] * 2 + [pltpu.VMEM((MODES, MODES), F32)],
        [VMEM] * 3,
        flops=800_000_000,
    )
    block_shape, half_shape = (MODES, MODES), (MODES, MODES2)
    early_blocks, early_outer, early_within = call(
        early_kernel,
        (present, highs, lows, self_block, packed[0], *[fetched[slot] for slot in EARLY]),
        [SMEM] + [VMEM] * (4 + len(EARLY)),
        [pltpu.VMEM((len(EARLY), *block_shape), F32)] + [pltpu.VMEM(half_shape, F32)] * 2,
        [VMEM] * 3,
        [
            pltpu.VMEM((MODES, len(EARLY) * MODES), F32),
            pltpu.VMEM((len(EARLY) * MODES, MODES2), F32),
        ],
        flops=200_000_000,
    )
    late_blocks, half = call(
        late_kernel,
        (present, highs, lows, early_outer, early_within, *[fetched[slot] for slot in LATE]),
        [SMEM] + [VMEM] * (4 + len(LATE)),
        [pltpu.VMEM((len(LATE), *block_shape), F32), pltpu.VMEM((MODES, 3 * MODES2), F32)],
        [VMEM] * 2,
        [
            pltpu.VMEM((MODES, (len(LATE) - 1) * MODES), F32),
            pltpu.VMEM(((len(LATE) - 1) * MODES, MODES2), F32),
        ],
        flops=200_000_000,
    )
    partner_half = near(lax.ppermute(half, "sub", [(i, i ^ 1) for i in range(SUBS)]))
    partner = fetched[EXCHANGES.index(("column", 0))]
    left, own_terms, blocks = call(
        left_kernel,
        (packed[0], partner, half, self_block, early_blocks, late_blocks),
        [VMEM] * 6,
        [
            pltpu.VMEM((2, MODES, MODES), BF16),
            pltpu.VMEM((MODES, 3 * MODES2), F32),
            jax.ShapeDtypeStruct((1, DIRS + 1, MODES, MODES), F32),
        ],
        [VMEM, VMEM, HBM],
        [pltpu.VMEM((2, MODES, MODES), F32), pltpu.SemaphoreType.DMA((DIRS + 1,))],
        flops=150_000_000,
    )
    (terms,) = call(
        term_kernel,
        (left, partner_half, own_terms),
        [VMEM] * 3,
        [pltpu.VMEM((CHIPS, ROWS, 3 * MODES2), F32)],
        [VMEM],
        flops=150_000_000,
    )
    chips = [[core + 2 * chip for chip in range(CHIPS)] for core in range(2)]
    parts = near(lax.all_to_all(terms, "sub", 0, 0, axis_index_groups=chips))
    (own_rows,) = call(
        sum_kernel, (parts,), [VMEM], [jax.ShapeDtypeStruct((1, 3, ROWS, MODES2), F32)], [VMEM]
    )
    return (blocks, own_rows)


def solution(mesh):
    both = ("group", "sub")
    return jax.shard_map(
        body,
        mesh=mesh,
        in_specs=(
            P(both, None, None, None),
            P(both, None),
            P(both, None),
            P(both, None),
            P(both, None),
            P(both, None),
            P(both, None),
        ),
        out_specs=(P(both, None, None, None), P("group", None, "sub", None)),
        check_vma=False,
    )
```
